32 devices in a mesh: depth: 4 (over z), tile: 8 (over y, x, core).
Axes of the slice: x: 2, y: 2, z: 4, core: 2. Of those that a mesh axis runs over, the one named last changes fastest.
Arguments:
- patches: float32 [512, 64, 1024], P('tile', 'depth'), may hold values from 0.1 to 10
- patch_slot: int32 [512], P('tile'), may hold values from 0 to 511, as said below
Outputs:
- image: float32 [8, 64, 4, 1024], P('tile', 'depth')
The draws below stay inside these ranges and needn't reach their ends.
Inputs may be any that keep to these rules, and one draw needn't show every extreme that they name: patch_slot is a permutation of the slots. Device s of tile (patches s * 64 to (s + 1) * 64 - 1) sends to owner t a number that depends only on (t - s) mod 8: one such difference, drawn from the seed, carries 24 patches, two carry none, the others 64 // 8. Every owner receives 64 patches.
All inputs are finite; a program needn't handle non-finite values.
Results may differ from the reference program's by a relative error of at most 0.00002.
Values sent between devices are 32-bit elements; how exact they have to be, the bound alone decides.
A program may use at most 128 MiB of HBM per device.

```python
import math
import jax
import jax.numpy as jnp
from jax import lax

PIX = 1024
PATCH_DEV = 64
NZ = 64
PATCHES = 512
N_TILE = 8


def draw_patch_slot(key, part):
    tiles = N_TILE
    per = PATCH_DEV
    share = per // tiles
    first_key, second_key, third_key = jax.random.split(key, 3)
    order = jax.random.permutation(first_key, tiles)
    weights = jnp.full((tiles,), share, jnp.int32)
    weights = weights.at[order[0]].set(3 * share).at[order[1]].set(0).at[order[2]].set(0)
    sources = jnp.arange(tiles, dtype=jnp.int32)[:, None]
    targets = jnp.arange(tiles, dtype=jnp.int32)[None, :]
    counts = weights[(targets - sources) % tiles]
    base = jnp.cumsum(counts, axis=0) - counts
    running = jnp.cumsum(weights)
    places = jnp.arange(per, dtype=jnp.int32)
    shifts = jnp.sum((places[:, None] >= running[None, :]).astype(jnp.int32), axis=1)
    within = places - (running - weights)[shifts]
    owners = (sources + shifts[None, :]) % tiles
    ranking = jnp.take_along_axis(base, owners, axis=1) + within[None, :]
    shuffles = jax.vmap(lambda sub: jax.random.permutation(sub, per))(jax.random.split(second_key, tiles))
    offsets = shuffles[owners, ranking]
    slots = owners * per + offsets
    reorder = jax.vmap(lambda sub: jax.random.permutation(sub, per))(jax.random.split(third_key, tiles))
    return jnp.take_along_axis(slots, reorder, axis=1).reshape(tiles * per).astype(jnp.int32)


def block_scale(stream_key, shape, cuts, least, largest):
    gain, own = 1.0, jax.random.fold_in(stream_key, 6)
    for axis_at, shards_of in cuts:
        heights = jnp.exp(jax.random.uniform(jax.random.fold_in(own, axis_at), (shards_of,), jnp.float32, least / len(cuts), largest / len(cuts)))
        gain = gain * jnp.repeat(heights, shape[axis_at] // shards_of).reshape([-1 if axis == axis_at else 1 for axis in range(len(shape))])
    return gain


def setup_inputs(seed: int = 0) -> dict:
    key_list = jax.random.split(jax.random.key(seed), 3)
    patches = jnp.clip(jnp.exp(math.log(10.0) - 4.6051702 * jax.random.uniform(key_list[0], (PATCHES, NZ, PIX), jnp.float32) ** block_scale(key_list[0], (PATCHES, NZ, PIX), ((0, 8), (1, 4)), -0.2, 0.2)), 0.1, 10.0)
    patch_slot = draw_patch_slot(jax.random.fold_in(key_list[2], 71), 0)
    return {"patches": patches, "patch_slot": patch_slot}


def shade_rays(padded, depth_total):
    level = padded[:, 1:-1]
    slope = (padded[:, 2:] - padded[:, :-2]) * 0.5
    sigma = 0.6 * jnp.exp(-(level - 0.5) ** 2) + 0.4 * jnp.exp(-2.0 * (level + 1.0) ** 2) + 0.3 * slope * slope
    optical = sigma * (2.0 / depth_total)
    depth_sum = jnp.cumsum(optical, axis=1)
    weight = jnp.exp(-(depth_sum - optical)) * (1.0 - jnp.exp(-optical))
    lighting = weight / (1.0 + slope * slope)
    red = jnp.sum(lighting * jax.nn.sigmoid(2.0 * level), axis=1)
    green = jnp.sum(lighting * jnp.exp(-level * level), axis=1)
    blue = jnp.sum(lighting * jax.nn.sigmoid(-2.0 * level), axis=1)
    remain = jnp.exp(-depth_sum[:, -1])
    return jnp.stack([red, green, blue, remain], axis=1)


def render_group(density):
    level = jnp.log(density)
    padded = jnp.pad(level, ((0, 0), (1, 1), (0, 0)))
    return shade_rays(padded, NZ)


def reference(patches, patch_slot):
    groups = patches.reshape(N_TILE, PATCH_DEV, NZ, PIX)
    rendered = lax.map(render_group, groups).reshape(PATCHES, 4, PIX)
    placed = jnp.zeros_like(rendered).at[patch_slot].set(rendered)
    color = placed[:, :3]
    alpha = 1.0 - placed[:, 3:]
    return jnp.concatenate([color, alpha], axis=1).reshape(N_TILE, PATCH_DEV, 4, PIX)
```

```python
import functools
import math

import jax
import jax.numpy as jnp
from jax import lax
from jax.experimental import pallas as pl
from jax.experimental.pallas import tpu as pltpu
from jax.sharding import PartitionSpec as P

LANES = 128
ROWS = 8
GROUP = 16
HIGHEST = lax.Precision.HIGHEST


def render_kernel(
    depths, tiles, per, cells, pix, cap, pad,
    patches, slot, out,
    grid, low, high, lay, got, packed, labels, recv, marks, final, back,
    load_sem, halo_send, halo_recv, lay_send, lay_recv, tile_send, tile_recv, mark_send, mark_recv,
    back_send, back_recv,
):
    z = lax.axis_index("depth")
    me = lax.axis_index("tile")
    wide = depths * LANES
    chunks = pix // wide
    groups = per // GROUP
    share = per // depths
    scale = 2.0 / (cells * depths)

    def other(delta):
        return lax.rem(z + delta, depths)

    def peer(delta):
        return lax.rem(me + delta, tiles)

    def load(c, k):
        lanes = pl.ds(c * wide, wide)
        return pltpu.make_async_copy(patches.at[:, k, lanes], grid.at[k, c], load_sem.at[c, k])

    def halo_up(c, g):
        rows = pl.ds(pl.multiple_of(g * GROUP, GROUP), GROUP)
        return pltpu.make_async_remote_copy(
            grid.at[cells - 1, c, rows], low.at[c, rows], halo_send.at[0, c, g], halo_recv.at[0, c, g],
            device_id={"depth": z + 1}, device_id_type=pl.DeviceIdType.MESH)

    def halo_down(c, g):
        rows = pl.ds(pl.multiple_of(g * GROUP, GROUP), GROUP)
        return pltpu.make_async_remote_copy(
            grid.at[0, c, rows], high.at[c, rows], halo_send.at[1, c, g], halo_recv.at[1, c, g],
            device_id={"depth": z - 1}, device_id_type=pl.DeviceIdType.MESH)

    def send_lay(c, g, delta):
        rows = pl.ds(pl.multiple_of(g * GROUP, GROUP), GROUP)
        to = other(delta)
        return pltpu.make_async_remote_copy(
            lay.at[c, to, rows], got.at[c, z, rows], lay_send.at[c, g, to], lay_recv.at[c, g, z],
            device_id={"depth": to}, device_id_type=pl.DeviceIdType.MESH)

    def take_lay(c, g, delta):
        rows = pl.ds(pl.multiple_of(g * GROUP, GROUP), GROUP)
        src = other(delta)
        return pltpu.make_async_remote_copy(
            lay.at[c, src, rows], got.at[c, src, rows], lay_send.at[c, g, src], lay_recv.at[c, g, src],
            device_id={"depth": src}, device_id_type=pl.DeviceIdType.MESH)

    def send_tile(c, delta):
        to = peer(delta)
        return pltpu.make_async_remote_copy(
            packed.at[c, to], recv.at[c, me], tile_send.at[c, to], tile_recv.at[c, me],
            device_id={"tile": to}, device_id_type=pl.DeviceIdType.MESH)

    def take_tile(c, src):
        return pltpu.make_async_remote_copy(
            packed.at[c, src], recv.at[c, src], tile_send.at[c, src], tile_recv.at[c, src],
            device_id={"tile": src}, device_id_type=pl.DeviceIdType.MESH)

    def send_mark(delta):
        to = peer(delta)
        return pltpu.make_async_remote_copy(
            labels.at[to], marks.at[me], mark_send.at[to], mark_recv.at[me],
            device_id={"tile": to}, device_id_type=pl.DeviceIdType.MESH)

    def take_mark(src):
        return pltpu.make_async_remote_copy(
            labels.at[src], marks.at[src], mark_send.at[src], mark_recv.at[src],
            device_id={"tile": src}, device_id_type=pl.DeviceIdType.MESH)

    def send_back(c, delta):
        to = other(delta)
        return pltpu.make_async_remote_copy(
            final.at[c, to], back.at[c, z], back_send.at[c, to], back_recv.at[c, z],
            device_id={"depth": to}, device_id_type=pl.DeviceIdType.MESH)

    def take_back(c, delta):
        src = other(delta)
        return pltpu.make_async_remote_copy(
            final.at[c, src], back.at[c, src], back_send.at[c, src], back_recv.at[c, src],
            device_id={"depth": src}, device_id_type=pl.DeviceIdType.MESH)

    order = [0, cells - 1] + list(range(1, cells - 1))
    for c in range(chunks):
        for k in order[:2]:
            load(c, k).start()
    for c in range(chunks):
        for k in order[2:]:
            load(c, k).start()

    barrier = pltpu.get_barrier_semaphore()
    for delta in range(1, depths):
        pl.semaphore_signal(barrier, inc=1, device_id={"depth": other(delta)}, device_id_type=pl.DeviceIdType.MESH)

    @pl.loop(1, tiles)
    def _(delta):
        pl.semaphore_signal(barrier, inc=1, device_id={"tile": peer(delta)}, device_id_type=pl.DeviceIdType.MESH)

    @pl.when(z == 0)
    def _():
        low[...] = jnp.ones_like(low)

    @pl.when(z == depths - 1)
    def _():
        high[...] = jnp.ones_like(high)

    bits = int(math.log2(per))
    line = lax.broadcasted_iota(jnp.int32, (per, per), 0)
    column = lax.broadcasted_iota(jnp.int32, (per, per), 1)
    slot_row = jnp.broadcast_to(slot[...], (per, per))
    slot_col = jnp.broadcast_to(
        jnp.sum(jnp.where(line == column, slot_row, 0), axis=1, keepdims=True), (per, per))
    owner_row = lax.shift_right_logical(slot_row, bits)
    owner_col = lax.shift_right_logical(slot_col, bits)
    same = owner_row == owner_col
    rank_row = jnp.sum(jnp.where(same & (line < column), 1, 0), axis=0, keepdims=True)
    rank_col = jnp.sum(jnp.where(same & (column < line), 1, 0), axis=1, keepdims=True)
    target = owner_row[:1] * pad + rank_row
    place = lax.broadcasted_iota(jnp.int32, (tiles * pad, per), 0)
    spread = (place == jnp.broadcast_to(target, (tiles * pad, per))).astype(jnp.float32)
    offset = (slot_col[:, :1] & (per - 1)) + 1
    spot = lax.broadcasted_iota(jnp.int32, (per, LANES), 1)
    tagged = jnp.where(spot == jnp.broadcast_to(rank_col, (per, LANES)),
                       jnp.broadcast_to(offset, (per, LANES)), 0).astype(jnp.float32)
    holder = lax.shift_right_logical(lax.broadcasted_iota(jnp.int32, (tiles * ROWS, per), 0), 3)
    mine = (holder == jnp.broadcast_to(owner_row[:1], (tiles * ROWS, per))).astype(jnp.float32)
    named = jnp.dot(mine, tagged, precision=HIGHEST, preferred_element_type=jnp.float32) - 1.0
    labels[...] = named.reshape(tiles, ROWS, LANES)

    pl.semaphore_wait(barrier, depths + tiles - 2)

    for c in range(chunks):
        for k in order[:2]:
            load(c, k).wait()
        for g in range(groups):
            @pl.when(z < depths - 1)
            def _():
                halo_up(c, g).start()

            @pl.when(z > 0)
            def _():
                halo_down(c, g).start()

    @pl.loop(1, tiles)
    def _(delta):
        send_mark(delta).start()

    marks[me] = labels[me]

    for c in range(chunks):
        for k in order[2:]:
            load(c, k).wait()

        @pl.loop(0, groups)
        def _(g):
            @pl.when(z > 0)
            def _():
                halo_up(c, g).wait_recv()

            @pl.when(z < depths - 1)
            def _():
                halo_down(c, g).wait_recv()

            @pl.loop(0, GROUP // ROWS)
            def _(half):
                rows = pl.ds(pl.multiple_of(g * GROUP + half * ROWS, ROWS), ROWS)
                before = jnp.log(low[c, rows])
                density = grid[0, c, rows]
                level = jnp.log(density)
                remain = red = green = blue = None
                for k in range(cells):
                    later = grid[k + 1, c, rows] if k + 1 < cells else high[c, rows]
                    after = jnp.log(later)
                    slope = (after - before) * 0.5
                    steep = slope * slope
                    bell = jnp.exp(-(level * level))
                    square = density * density
                    dim = 1.0 + steep
                    both = dim * (1.0 + square)
                    inverse = 1.0 / (both * square)
                    tail = bell * (inverse * both)
                    tau = (
                        (0.6 * math.exp(-0.25) * scale) * (bell * density)
                        + (0.4 * math.exp(-2.0) * scale) * (tail * tail)
                        + (0.3 * scale) * steep
                    )
                    pass_on = jnp.exp(-tau)
                    lost = 1.0 - pass_on
                    weight = lost if remain is None else remain * lost
                    lit = weight * (inverse * square)
                    r, gr, b = lit * square, lit * (1.0 + square) * bell, lit
                    if remain is None:
                        remain, red, green, blue = pass_on, r, gr, b
                    else:
                        remain, red, green, blue = remain * pass_on, red + r, green + gr, blue + b
                    before, level, density = level, after, later
                for j in range(depths):
                    for ch, value in enumerate((red, green, blue, remain)):
                        lay[c, j, rows, ch * LANES:(ch + 1) * LANES] = value[:, j * LANES:(j + 1) * LANES]

            for delta in range(1, depths):
                send_lay(c, g, delta).start()

    for c in range(chunks):
        got[c, z] = lay[c, z]

        @pl.loop(0, groups)
        def _(g):
            for delta in range(1, depths):
                take_lay(c, g, delta).wait_recv()

        red = [got[c, 0, :, ch * LANES:(ch + 1) * LANES] for ch in range(4)]
        for s in range(1, depths):
            for ch in range(3):
                red[ch] = red[ch] + red[3] * got[c, s, :, ch * LANES:(ch + 1) * LANES]
            red[3] = red[3] * got[c, s, :, 3 * LANES:]
        red[3] = 1.0 - red[3]
        for ch in range(4):
            block = jnp.dot(spread, red[ch], precision=HIGHEST, preferred_element_type=jnp.float32)
            packed[c, :, :, ch * LANES:(ch + 1) * LANES] = block.reshape(tiles, pad, LANES)

        @pl.loop(1, tiles)
        def _(delta):
            send_tile(c, delta).start()

        recv[c, me] = packed[c, me]

    number = lax.broadcasted_iota(jnp.int32, (per, pad), 0).astype(jnp.float32)
    for c in range(chunks):
        if c == 0:
            @pl.loop(1, tiles)
            def _(delta):
                take_mark(peer(delta)).wait_recv()

        @pl.loop(1, tiles)
        def _(delta):
            take_tile(c, peer(delta)).wait_recv()

        total = jnp.zeros((per, 4 * LANES), jnp.float32)
        for s in range(tiles):
            pick = (number == jnp.broadcast_to(marks[s, 0:1, 0:pad], (per, pad))).astype(jnp.float32)
            total = total + jnp.dot(pick, recv[c, s], precision=HIGHEST, preferred_element_type=jnp.float32)
        final[c] = total.reshape(depths, share, 4 * LANES)
        for delta in range(1, depths):
            send_back(c, delta).start()
        back[c, z] = final[c, z]

    for c in range(chunks):
        for delta in range(1, depths):
            take_back(c, delta).wait_recv()
        for s in range(depths):
            for ch in range(4):
                start = ch * pix + c * wide + s * LANES
                out[:, start:start + LANES] = back[c, s, :, ch * LANES:(ch + 1) * LANES]

    for c in range(chunks):
        for g in range(groups):
            @pl.when(z < depths - 1)
            def _():
                halo_up(c, g).wait_send()

            @pl.when(z > 0)
            def _():
                halo_down(c, g).wait_send()

            for delta in range(1, depths):
                send_lay(c, g, delta).wait_send()

        @pl.loop(1, tiles)
        def _(delta):
            send_tile(c, delta).wait_send()

        for delta in range(1, depths):
            send_back(c, delta).wait_send()

    @pl.loop(1, tiles)
    def _(delta):
        send_mark(delta).wait_send()


def local(patches, patch_slot):
    per, cells, pix = patches.shape
    depths, tiles = lax.axis_size("depth"), lax.axis_size("tile")
    cap = 3 * per // tiles
    pad = -(-cap // ROWS) * ROWS
    wide = depths * LANES
    chunks, groups, share = pix // wide, per // GROUP, per // depths
    row = 4 * LANES
    f32 = jnp.float32
    dma = pltpu.SemaphoreType.DMA
    image = pl.pallas_call(
        functools.partial(render_kernel, depths, tiles, per, cells, pix, cap, pad),
        out_shape=jax.ShapeDtypeStruct((share, 4 * pix), f32),
        in_specs=[pl.BlockSpec(memory_space=pl.ANY), pl.BlockSpec(memory_space=pltpu.VMEM)],
        out_specs=pl.BlockSpec(memory_space=pltpu.VMEM),
        scratch_shapes=[
            pltpu.VMEM((cells, chunks, per, wide), f32),
            pltpu.VMEM((chunks, per, wide), f32),
            pltpu.VMEM((chunks, per, wide), f32),
            pltpu.VMEM((chunks, depths, per, row), f32),
            pltpu.VMEM((chunks, depths, per, row), f32),
            pltpu.VMEM((chunks, tiles, pad, row), f32),
            pltpu.VMEM((tiles, ROWS, LANES), f32),
            pltpu.VMEM((chunks, tiles, pad, row), f32),
            pltpu.VMEM((tiles, ROWS, LANES), f32),
            pltpu.VMEM((chunks, depths, share, row), f32),
            pltpu.VMEM((chunks, depths, share, row), f32),
            dma((chunks, cells)),
            dma((2, chunks, groups)), dma((2, chunks, groups)),
            dma((chunks, groups, depths)), dma((chunks, groups, depths)),
            dma((chunks, tiles)), dma((chunks, tiles)),
            dma((tiles,)), dma((tiles,)),
            dma((chunks, depths)), dma((chunks, depths)),
        ],
        compiler_params=pltpu.CompilerParams(
            collective_id=0, has_side_effects=True, vmem_limit_bytes=48 * 1024 * 1024),
        name="render",
    )(patches, patch_slot.reshape(1, per))
    return image.reshape(1, share, 4, pix)


def solution(mesh):
    return jax.shard_map(
        local,
        mesh=mesh,
        in_specs=(P("tile", "depth", None), P("tile")),
        out_specs=P("tile", "depth", None, None),
        check_vma=False,
    )
```
